32 devices in a mesh: frames: 16 (over z, y, core), heads: 2 (over x).
Axes of the slice: x: 2, y: 2, z: 4, core: 2. Of those that a mesh axis runs over, the one named last changes fastest.
Arguments:
- queries: bfloat16 [4096, 2048], P('frames', 'heads'), may hold values from -8 to 8
- keys: bfloat16 [4096, 2048], P('frames', 'heads'), may hold values from -8 to 8
- values: bfloat16 [4096, 2048], P('frames', 'heads'), may hold values from -6 to 6
- out_grad: bfloat16 [4096, 2048], P('frames', 'heads'), may hold values from -6 to 6
- out_weight: bfloat16 [2048, 2048], P('heads'), may hold values from -0.125 to 0.125
Outputs:
- mixed: bfloat16 [4096, 2048], P('frames', 'heads')
- query_grad: bfloat16 [4096, 2048], P('frames', 'heads')
- key_grad: bfloat16 [4096, 2048], P('frames', 'heads')
- value_grad: bfloat16 [4096, 2048], P('frames', 'heads')
- weight_grad: bfloat16 [2048, 2048], P('heads', 'frames')
The draws below stay inside these ranges and needn't reach their ends.
All inputs are finite; a program needn't handle non-finite values.
Results may differ from the reference program's by a relative error of at most 0.014.
Values may be sent and summed in bfloat16 or wider, within the bound.
No kernel may reach another device: no remote copies, remote signals or barrier semaphores. Data moves between devices by JAX's collectives and lax.ppermute only.
A program may use at most 128 MiB of HBM per device.

```python
import jax
import jax.numpy as jnp
from jax import lax

D = 2048
HEADS = 16
HEAD_DIM = 128
REGIONS = 128
WIN = 8
FR_DEV = 2
FRAMES = 32
TOKENS = 4096
N_FRAMES = 16
N_HEADS = 2


def paired_rows(key):
    base_queries = 2.0 * jax.random.truncated_normal(jax.random.fold_in(key, 101), -4.0, 4.0, (TOKENS, D), jnp.float32)
    base_keys = 2.0 * jax.random.truncated_normal(jax.random.fold_in(key, 102), -4.0, 4.0, (TOKENS, D), jnp.float32)
    return (base_queries, base_keys)


def draw_queries(key, part):
    return paired_rows(key)[0].astype(jnp.bfloat16)


def draw_keys(key, part):
    return paired_rows(key)[1].astype(jnp.bfloat16)


def strengthened(array, rng, source, target, blocks, factor):
    owner, partner = [(jnp.arange(array.shape[position]) // (array.shape[position] // blocks)).reshape([-1 if axis == position else 1 for axis in range(array.ndim)]) for position in (source, target)]
    chosen = jax.random.permutation(rng, blocks)[partner]
    strong = (owner == chosen) | (owner == (partner + blocks // 2) % blocks)
    return jnp.where(strong, factor * array, array)


def steps_of(rng, extent, cuts, low, largest):
    def one(position, parts):
        heights = jax.random.uniform(jax.random.fold_in(jax.random.fold_in(rng, 6), position), (parts,), jnp.float32, low / len(cuts), largest / len(cuts))
        return jnp.repeat(jnp.exp(heights), extent[position] // parts).reshape((-1,) + (1,) * (len(extent) - position - 1))

    loudness = one(*cuts[0])
    for cut in cuts[1:]:
        loudness = loudness * one(*cut)
    return loudness


def noise(stream_key, dims, spread, reach, shards=(), kind=jnp.bfloat16):
    array = jax.random.normal(stream_key, dims, jnp.float32) * spread
    if len(shards) > 0:
        array = steps_of(stream_key, dims, shards, -0.22, 0.18) * array
    return jnp.clip(array, min=-reach, max=reach).astype(kind)


def bell_draw_with(rng, shape, scale, limit, cuts, heavy, kind=jnp.bfloat16):
    drawn = scale * jax.random.normal(rng, shape, jnp.float32)
    if cuts:
        drawn = drawn * steps_of(rng, shape, cuts, -0.22, 0.18)
    return jnp.clip(strengthened(drawn, jax.random.fold_in(rng, 3), *heavy), -limit, limit).astype(kind)


def setup_inputs(seed: int = 0) -> dict:
    key_of = jax.random.split(jax.random.key(seed), 6)
    return {
        "queries": draw_queries(jax.random.fold_in(key_of[5], 71), 0),
        "keys": draw_keys(jax.random.fold_in(key_of[5], 71), 0),
        "values": noise(key_of[2], (TOKENS, D), 1.0, 6.0, ((0, 16), (1, 2))),
        "out_grad": bell_draw_with(key_of[3], (TOKENS, D), 1.0, 6.0, ((0, 16), (1, 2)), (0, 1, 16, 2.0)),
        "out_weight": noise(key_of[4], (D, D), D ** -0.5, 0.125, ((0, 2),)),
    }


def rounded(value):
    return lax.optimization_barrier(value.astype(jnp.bfloat16)).astype(jnp.float32)


def reference(queries, keys, values, out_grad, out_weight):
    block = FR_DEV * REGIONS
    margin = WIN * REGIONS
    span = block + 2 * margin
    scale = HEAD_DIM ** -0.5
    group = HEADS // N_HEADS
    padded_keys = jnp.pad(keys, ((margin, margin), (0, 0)))
    padded_values = jnp.pad(values, ((margin, margin), (0, 0)))
    weight_rows = out_weight.astype(jnp.float32).reshape(N_HEADS, group * HEAD_DIM, D)

    def advance(carry, index):
        key_acc, value_acc, weight_acc = carry
        start = index * block
        query_block = lax.dynamic_slice_in_dim(queries, start, block, 0)
        key_block = lax.dynamic_slice_in_dim(padded_keys, start, span, 0)
        value_block = lax.dynamic_slice_in_dim(padded_values, start, span, 0)
        grad_block = lax.dynamic_slice_in_dim(out_grad, start, block, 0)
        query_frame = index * FR_DEV + jnp.arange(block, dtype=jnp.int32) // REGIONS
        key_frame = index * FR_DEV - WIN + jnp.arange(span, dtype=jnp.int32) // REGIONS
        near = (jnp.abs(query_frame[:, None] - key_frame[None, :]) <= WIN) & (key_frame >= 0)[None, :] & (key_frame < FRAMES)[None, :]
        query_heads = query_block.astype(jnp.float32).reshape(block, HEADS, HEAD_DIM)
        key_heads = key_block.astype(jnp.float32).reshape(span, HEADS, HEAD_DIM)
        value_heads = value_block.astype(jnp.float32).reshape(span, HEADS, HEAD_DIM)
        scores = jnp.einsum("qhd,khd->hqk", query_heads, key_heads) * scale
        scores = jnp.where(near[None], scores, -jnp.inf)
        top = jnp.max(scores, axis=-1, keepdims=True)
        expo = jnp.where(near[None], jnp.exp(scores - top), 0.0)
        probs = expo / jnp.sum(expo, axis=-1, keepdims=True)
        weights = rounded(probs)
        attn = jnp.einsum("hqk,khd->qhd", weights, value_heads).reshape(block, D).astype(jnp.bfloat16)
        pieces = jnp.einsum("tgc,gcd->gtd", attn.astype(jnp.float32).reshape(block, N_HEADS, group * HEAD_DIM), weight_rows)
        mixed = jnp.sum(rounded(pieces), axis=0).astype(jnp.bfloat16)
        grad_attn = jnp.dot(grad_block, out_weight.T, preferred_element_type=jnp.float32).astype(jnp.bfloat16)
        grad_heads = grad_attn.astype(jnp.float32).reshape(block, HEADS, HEAD_DIM)
        dprob = jnp.einsum("qhd,khd->hqk", grad_heads, value_heads)
        delta = jnp.sum(probs * dprob, axis=-1, keepdims=True)
        dscore = rounded(probs * (dprob - delta) * scale)
        query_grad = jnp.einsum("hqk,khd->qhd", dscore, key_heads).reshape(block, D).astype(jnp.bfloat16)
        key_part = jnp.einsum("hqk,qhd->khd", dscore, query_heads).reshape(span, D)
        value_part = jnp.einsum("hqk,qhd->khd", weights, grad_heads).reshape(span, D)
        key_acc = lax.dynamic_update_slice_in_dim(key_acc, lax.dynamic_slice_in_dim(key_acc, start, span, 0) + key_part, start, 0)
        value_acc = lax.dynamic_update_slice_in_dim(value_acc, lax.dynamic_slice_in_dim(value_acc, start, span, 0) + value_part, start, 0)
        weight_acc = weight_acc + jnp.dot(attn.T, grad_block, preferred_element_type=jnp.float32)
        return (key_acc, value_acc, weight_acc), (mixed, query_grad)

    start_acc = jnp.zeros((TOKENS + 2 * margin, D), jnp.float32)
    carry = (start_acc, start_acc, jnp.zeros((D, D), jnp.float32))
    carry, (mixed, query_grad) = lax.scan(advance, carry, jnp.arange(N_FRAMES, dtype=jnp.int32))
    key_acc, value_acc, weight_acc = carry
    key_grad = key_acc[margin:margin + TOKENS].astype(jnp.bfloat16)
    value_grad = value_acc[margin:margin + TOKENS].astype(jnp.bfloat16)
    return (mixed.reshape(TOKENS, D), query_grad.reshape(TOKENS, D), key_grad, value_grad, weight_acc.astype(jnp.bfloat16))
```

```python
import functools

import jax, jax.numpy as jnp
from jax import lax
from jax.experimental import pallas as pl
from jax.experimental.pallas import tpu as pltpu
from jax.sharding import Mesh
from jax.sharding import PartitionSpec as P

HEAD_DIM=128; REGIONS=128; WIN=8; FR_DEV=2
ROWS=FR_DEV*REGIONS
NEG=-1e30
NT=(((1,),(1,)),((),()))
NN=(((1,),(0,)),((),()))
LOG2E=1.4426950408889634

def attend_kernel(cfg, place_ref, *refs):
    group, reach, radius, devices = cfg
    blocks = 2*radius+1
    kv_refs = refs[:blocks]
    q_ref, g_ref = refs[blocks:blocks+2]
    attn_ref, dq_ref = refs[blocks+2:blocks+4]
    out_refs = refs[blocks+4:2*blocks+4]
    kw, vw, kt, vt, s_sc, dp_sc, e_sc, dk, dv = refs[2*blocks+4:]
    mine = place_ref[0]; block = place_ref[1]
    scale = HEAD_DIM ** -0.5
    chunks = 2*reach+1
    dk[...] = jnp.zeros_like(dk)
    dv[...] = jnp.zeros_like(dv)
    vt[HEAD_DIM:, :] = jnp.ones((vt.shape[0]-HEAD_DIM, vt.shape[1]), vt.dtype)
    for b in range(blocks):
        def load(slot, _):
            src = pl.multiple_of((slot ^ mine) * ROWS, ROWS)
            dst = pl.multiple_of((b*group + slot) * ROWS, ROWS)
            k = kv_refs[b][pl.ds(src, ROWS), :HEAD_DIM]
            v = kv_refs[b][pl.ds(src, ROWS), HEAD_DIM:]
            kw[pl.ds(dst, ROWS), :] = k
            vw[pl.ds(dst, ROWS), :] = v
            kt[:, pl.ds(dst, ROWS)] = k.T
            vt[:HEAD_DIM, pl.ds(dst, ROWS)] = v.T
            return 0
        lax.fori_loop(0, group, load, 0)
    key_frame = lax.broadcasted_iota(jnp.int32, (ROWS, ROWS), 0)//REGIONS
    query_frame = lax.broadcasted_iota(jnp.int32, (ROWS, ROWS), 1)//REGIONS

    def tile(s, _):
        slot = s ^ mine
        first = slot + radius*group - reach
        here = pl.ds(pl.multiple_of(s*ROWS, ROWS), ROWS)
        q = q_ref[here, :]
        g = g_ref[here, :]
        top = jnp.full((1, ROWS), NEG, jnp.float32)
        for c in range(chunks):
            rows = pl.ds(pl.multiple_of((first+c)*ROWS, ROWS), ROWS)
            st = lax.dot_general(kw[rows, :], q, NT, preferred_element_type=jnp.float32)*(scale*LOG2E)
            device = block*group + slot + (c-reach)
            live = (device >= 0) & (device < devices)
            shift = (c-reach)*FR_DEV
            if abs(shift)+FR_DEV-1 > WIN:
                near = jnp.abs(shift + key_frame - query_frame) <= WIN
                st = jnp.where(near & live, st, NEG)
            elif c != reach:
                st = jnp.where(live, st, NEG)
            s_sc[pl.ds(c*ROWS, ROWS), :] = st
            top = jnp.maximum(top, jnp.max(st, axis=0, keepdims=True))
            dp_sc[pl.ds(c*ROWS, ROWS), :] = lax.dot_general(vw[rows, :], g, NT, preferred_element_type=jnp.float32)
        ot = jnp.zeros((vt.shape[0], ROWS), jnp.float32)
        for c in range(chunks):
            rows = pl.ds(pl.multiple_of((first+c)*ROWS, ROWS), ROWS)
            e = jnp.exp2(s_sc[pl.ds(c*ROWS, ROWS), :] - top).astype(jnp.bfloat16)
            e_sc[pl.ds(c*ROWS, ROWS), :] = e
            ot = ot + lax.dot_general(vt[:, rows], e, NN, preferred_element_type=jnp.float32)
        inv = 1.0/ot[HEAD_DIM:HEAD_DIM+1, :]
        ot = ot[:HEAD_DIM, :]*inv
        delta = jnp.sum(ot*g.T.astype(jnp.float32), axis=0, keepdims=True)
        attn_ref[here, :] = ot.T.astype(jnp.bfloat16)
        inv_rows = jnp.broadcast_to(inv, (HEAD_DIM, ROWS)).T
        q_n = (q.astype(jnp.float32)*(inv_rows*scale)).astype(jnp.bfloat16)
        g_n = (g.astype(jnp.float32)*inv_rows).astype(jnp.bfloat16)
        dqt = jnp.zeros((HEAD_DIM, ROWS), jnp.float32)
        for c in range(chunks):
            rows = pl.ds(pl.multiple_of((first+c)*ROWS, ROWS), ROWS)
            e = e_sc[pl.ds(c*ROWS, ROWS), :]
            ds = (e.astype(jnp.float32)*(dp_sc[pl.ds(c*ROWS, ROWS), :]-delta)).astype(jnp.bfloat16)
            dqt = dqt + lax.dot_general(kt[:, rows], ds, NN, preferred_element_type=jnp.float32)
            dk[rows, :] += lax.dot_general(ds, q_n, NN, preferred_element_type=jnp.float32)
            dv[rows, :] += lax.dot_general(e, g_n, NN, preferred_element_type=jnp.float32)
        dq_ref[here, :] = (dqt*(inv*scale)).T.astype(jnp.bfloat16)
        return 0
    lax.fori_loop(0, group, tile, 0)
    for b in range(blocks):
        def store(slot, _):
            dst = pl.multiple_of((slot ^ mine) * ROWS, ROWS)
            src = pl.multiple_of((b*group + slot) * ROWS, ROWS)
            out_refs[b][pl.ds(dst, ROWS), :HEAD_DIM] = dk[pl.ds(src, ROWS), :].astype(out_refs[b].dtype)
            out_refs[b][pl.ds(dst, ROWS), HEAD_DIM:] = dv[pl.ds(src, ROWS), :].astype(out_refs[b].dtype)
            return 0
        lax.fori_loop(0, group, store, 0)

def attend(place, kv, q, g, *, group, reach, radius, devices):
    blocks = 2*radius+1
    size = group*ROWS
    span = blocks*size
    bf, f32 = jnp.bfloat16, jnp.float32
    S = jax.ShapeDtypeStruct
    wide = 2*HEAD_DIM
    pairs = size*(2*reach+1)*ROWS
    vm = pl.BlockSpec(memory_space=pltpu.VMEM)
    return pl.pallas_call(
        functools.partial(attend_kernel, (group, reach, radius, devices)),
        out_shape=[S((size, HEAD_DIM), bf)]*2+[S((size, wide), f32 if b == radius else bf) for b in range(blocks)],
        in_specs=[pl.BlockSpec(memory_space=pltpu.SMEM)]+[vm]*(blocks+2),
        out_specs=[vm]*(blocks+2),
        scratch_shapes=[
            pltpu.VMEM((span, HEAD_DIM), bf), pltpu.VMEM((span, HEAD_DIM), bf),
            pltpu.VMEM((HEAD_DIM, span), bf), pltpu.VMEM((HEAD_DIM+16, span), bf),
            pltpu.VMEM(((2*reach+1)*ROWS, ROWS), f32), pltpu.VMEM(((2*reach+1)*ROWS, ROWS), f32),
            pltpu.VMEM(((2*reach+1)*ROWS, ROWS), bf),
            pltpu.VMEM((span, HEAD_DIM), f32), pltpu.VMEM((span, HEAD_DIM), f32)],
        compiler_params=pltpu.CompilerParams(vmem_limit_bytes=48*1024*1024),
        cost_estimate=pl.CostEstimate(flops=12*pairs*HEAD_DIM, bytes_accessed=6*size*wide*2, transcendentals=pairs),
    )(place, *kv, q, g)


def swapped(piece, axis, mask):
    count = lax.axis_size(axis)
    return lax.ppermute(piece, axis, [(i, i ^ mask) for i in range(count)])


def moved(piece, axis, distance):
    count = lax.axis_size(axis)
    route = [(i, i + distance) for i in range(count) if 0 <= i + distance < count]
    return lax.ppermute(piece, axis, route)


def exchanged(slots, axis):
    return [slots[0]] + [swapped(slots[s], axis, s) for s in range(1, len(slots))]


def placed_in_order(slots, mine, axis):
    size = slots[0].shape[axis]
    shape = list(slots[0].shape)
    shape[axis] = size * len(slots)
    whole = jnp.zeros(shape, slots[0].dtype)
    for s, slot in enumerate(slots):
        whole = lax.dynamic_update_slice_in_dim(whole, slot, (mine ^ s) * size, axis)
    return whole


def gathered(block, axis, mine):
    count = lax.axis_size(axis)
    return placed_in_order([block] + [swapped(block, axis, s) for s in range(1, count)], mine, 1)


def body(queries, keys, values, out_grad, out_weight):
    bf, f32 = jnp.bfloat16, jnp.float32
    rows, width = queries.shape
    blocks, group, sides = (lax.axis_size(a) for a in ("block", "group", "heads"))
    block, mine, side = (lax.axis_index(a) for a in ("block", "group", "heads"))
    heads = width // HEAD_DIM // group
    part = heads * HEAD_DIM
    reach = (WIN + FR_DEV - 1) // FR_DEV
    radius = -(-reach // group)
    place = jnp.stack([mine, block]).astype(jnp.int32)

    def columns(array, s, head):
        return lax.dynamic_slice_in_dim(array, (mine ^ s) * part + head * HEAD_DIM, HEAD_DIM, 1)

    own_grad = gathered(out_grad, "heads", side)
    arrived = []
    for head in range(heads):
        slots = [
            jnp.concatenate([columns(a, s, head) for a in (keys, values, queries)], axis=1)
            for s in range(group)
        ]
        arrived.append(jnp.concatenate(exchanged(slots, "group"), axis=0))
    windows = []
    for head in range(heads):
        kv = arrived[head][:, : 2 * HEAD_DIM]
        windows.append([
            kv if d == 0 else moved(kv, "block", -d) for d in range(-radius, radius + 1)
        ])
    grad_attn = jnp.einsum("td,cd->tc", own_grad, out_weight, preferred_element_type=f32).astype(bf)
    grad_slots = exchanged(
        [lax.dynamic_slice_in_dim(grad_attn, (mine ^ s) * part, part, 1) for s in range(group)], "group"
    )
    grad_block = jnp.concatenate(grad_slots, axis=0)

    half = out_grad[None]
    whole = own_grad[None]
    bit = group // 2
    while bit:
        if bit > 1:
            other = swapped(half, "group", bit)
            half = jnp.stack([half, other], 1).reshape(-1, *half.shape[1:])
            flat = gathered(other.reshape(-1, other.shape[-1]), "heads", side)
            other = flat.reshape(*other.shape[:-1], -1)
        else:
            other = swapped(whole, "group", bit)
        whole = jnp.stack([whole, other], 1).reshape(-1, *whole.shape[1:])
        bit //= 2
    block_grad = whole.reshape(group * rows, -1)

    attn_pieces = [[] for _ in range(group)]
    query_pieces = [[] for _ in range(group)]
    key_pieces = [[] for _ in range(group)]
    value_pieces = [[] for _ in range(group)]
    attns = []
    for head in range(heads):
        q = arrived[head][:, 2 * HEAD_DIM :]
        g = grad_block[:, head * HEAD_DIM : (head + 1) * HEAD_DIM]
        attn, dq, *dkv = attend(
            place, windows[head], q, g, group=group, reach=reach, radius=radius, devices=blocks * group
        )
        attns.append(attn)
        total = dkv[radius]
        for d in range(-radius, radius + 1):
            if d != 0:
                total = total + moved(dkv[radius + d], "block", d).astype(f32)
        total = total.astype(bf)
        first = jnp.concatenate([attn, dq], axis=1)
        first = exchanged([first[s * rows : (s + 1) * rows] for s in range(group)], "group")
        second = exchanged([total[s * rows : (s + 1) * rows] for s in range(group)], "group")
        for s in range(group):
            attn_pieces[s].append(first[s][:, :HEAD_DIM])
            query_pieces[s].append(first[s][:, HEAD_DIM:])
            key_pieces[s].append(second[s][:, :HEAD_DIM])
            value_pieces[s].append(second[s][:, HEAD_DIM:])

    def finished(pieces):
        return placed_in_order([jnp.concatenate(p, axis=1) for p in pieces], mine, 1)

    partial = jnp.einsum(
        "tc,td->cd", jnp.concatenate(attns, axis=1), block_grad, preferred_element_type=f32
    )
    bit = 1
    partial = partial.reshape(part, blocks, -1)
    while bit < blocks:
        pairs = partial.reshape(part, partial.shape[1] // 2, 2, -1)
        own = (block // bit) % 2
        away = lax.dynamic_index_in_dim(pairs, 1 - own, 2, keepdims=False).astype(bf)
        kept = lax.dynamic_index_in_dim(pairs, own, 2, keepdims=False)
        partial = kept + swapped(away, "block", bit).astype(f32)
        bit *= 2
    partial = partial.reshape(part, -1).astype(bf)
    narrow = partial.shape[1] // group
    weight_grad = placed_in_order(
        exchanged(
            [lax.dynamic_slice_in_dim(partial, (mine ^ s) * narrow, narrow, 1) for s in range(group)],
            "group",
        ),
        mine,
        0,
    )
    product = jnp.dot(finished(attn_pieces), out_weight, preferred_element_type=f32).astype(bf)
    mixed = None
    for s in range(sides):
        share = lax.dynamic_slice_in_dim(product, (side ^ s) * width, width, 1)
        share = (swapped(share, "heads", s) if s else share).astype(f32)
        mixed = share if mixed is None else mixed + share
    return (
        mixed.astype(bf),
        finished(query_pieces),
        finished(key_pieces),
        finished(value_pieces),
        weight_grad,
    )


def solution(mesh):
    devices, sides = mesh.devices.shape
    reach = (WIN + FR_DEV - 1) // FR_DEV

    def run(queries, keys, values, out_grad, out_weight):
        heads = queries.shape[1] // sides // HEAD_DIM
        group = 1
        while 2 * group <= reach and heads % (2 * group) == 0 and devices % (2 * group) == 0:
            group *= 2
        fine = Mesh(
            mesh.devices.reshape(devices // group, group, sides), ("block", "group", "heads")
        )
        split = P(("block", "group"), "heads")
        return jax.shard_map(
            body,
            mesh=fine,
            in_specs=(split, split, split, split, P("heads", None)),
            out_specs=(split, split, split, split, P("heads", ("block", "group"))),
            check_vma=False,
        )(queries, keys, values, out_grad, out_weight)

    return run
```

```python
import functools

import jax
import jax.numpy as jnp
from jax import lax
from jax.experimental import pallas as pl
from jax.experimental.pallas import tpu as pltpu
from jax.sharding import Mesh
from jax.sharding import PartitionSpec as P


HEAD_DIM = 128
REGIONS = 128
WIN = 8
FR_DEV = 2
ROWS = FR_DEV * REGIONS
LOW = -1e30
LOG2E = 1.4426950408889634
PLAIN = (((1,), (0,)), ((), ()))
BF, F32 = jnp.bfloat16, jnp.float32
SMEM = pl.BlockSpec(memory_space=pltpu.SMEM)
VMEM = pl.BlockSpec(memory_space=pltpu.VMEM)
HBM = pl.BlockSpec(memory_space=pltpu.HBM)
PARAMS = pltpu.CompilerParams(vmem_limit_bytes=48 * 1024 * 1024)

PACK_PARAMS = pltpu.CompilerParams(vmem_limit_bytes=67043328)


def dot(a, b, dims=PLAIN):
    return lax.dot_general(a, b, dims, preferred_element_type=F32)


def aligned(start, size):
    return pl.ds(pl.multiple_of(start, size), size)


def attend_kernel(cfg, place_ref, *refs):
    group, reach, radius, devices, sets, filled = cfg
    blocks = 2 * radius + 1
    refs = list(refs)

    def take(count):
        head, refs[:] = refs[:count], refs[count:]
        return head

    kv_refs = [take(len(sets)) for _ in range(blocks)]
    qg_refs = take(group)
    take(filled)
    both_refs = take(group)
    (turned_ref,) = take(1)
    out_refs = take(blocks)
    kw, vw, kt, vt, s_sc, *rest = refs
    dp_scs, e_scs, (dk, dv) = rest[:2], rest[2:4], rest[4:]
    mine, block = place_ref[0], place_ref[1]
    scale = HEAD_DIM ** -0.5
    chunks = 2 * reach + 1
    dk[...] = jnp.zeros_like(dk)
    dv[...] = jnp.zeros_like(dv)
    vt[HEAD_DIM:, :] = jnp.ones((vt.shape[0] - HEAD_DIM, vt.shape[1]), vt.dtype)
    position = [radius]
    for d in range(1, radius + 1):
        for parity in range(2):
            position.append(radius + jnp.where((block // d) % 2 == parity, d, -d))
    for b in range(blocks):
        for part, members in enumerate(sets):
            for at, s in enumerate(members):
                there = aligned((position[b] * group + (s ^ mine)) * ROWS, ROWS)
                k = kv_refs[b][part][at * ROWS : (at + 1) * ROWS, :HEAD_DIM]
                v = kv_refs[b][part][at * ROWS : (at + 1) * ROWS, HEAD_DIM:]
                kw[there, :] = k
                vw[there, :] = v
                kt[:, there] = k.T
                vt[:HEAD_DIM, there] = v.T
    query_frame = lax.broadcasted_iota(jnp.int32, (1, ROWS), 1) // REGIONS

    def window(s, c):
        return aligned(((s ^ mine) + radius * group - reach + c) * ROWS, ROWS)

    def scores(s):
        qt = qg_refs[s][:, :HEAD_DIM].T
        top = jnp.full((1, ROWS), LOW, F32)
        biases = []
        for c in range(chunks):
            st = dot(kw[window(s, c), :], qt)
            s_sc[c * ROWS : (c + 1) * ROWS, :] = st
            device = block * group + (s ^ mine) + (c - reach)
            live = jnp.where((device >= 0) & (device < devices), 0.0, LOW)
            for f in range(FR_DEV):
                distance = (c - reach) * FR_DEV + f - query_frame
                bias = jnp.where(jnp.abs(distance) <= WIN, live, LOW)
                biases.append(bias)
                some = st[f * REGIONS : (f + 1) * REGIONS, :]
                top = jnp.maximum(top, jnp.max(some, axis=0, keepdims=True) * (scale * LOG2E) + bias)
        return [bias - top for bias in biases]

    def weigh(s, c, shifts, gt, ot):
        e_sc, dp_sc = e_scs[s % 2], dp_scs[s % 2]
        for f in range(FR_DEV):
            some = slice(c * ROWS + f * REGIONS, c * ROWS + (f + 1) * REGIONS)
            e_sc[some, :] = jnp.exp2(
                s_sc[some, :] * (scale * LOG2E) + shifts[c * FR_DEV + f]
            ).astype(BF)
        dp_sc[c * ROWS : (c + 1) * ROWS, :] = dot(vw[window(s, c), :], gt)
        return ot + dot(vt[:, window(s, c)], e_sc[c * ROWS : (c + 1) * ROWS, :])

    def settle(s, ot, gt):
        inv = 1.0 / ot[HEAD_DIM : HEAD_DIM + 1, :]
        ot = ot[:HEAD_DIM, :] * inv
        delta = jnp.sum(ot * gt.astype(F32), axis=0, keepdims=True)
        turned_ref[:, s * ROWS : (s + 1) * ROWS] = ot.astype(BF)
        both_refs[s][:, :HEAD_DIM] = ot.T.astype(BF)
        inv_rows = jnp.broadcast_to(inv, (HEAD_DIM, ROWS)).T
        q_n = (qg_refs[s][:, :HEAD_DIM].astype(F32) * (inv_rows * scale)).astype(BF)
        g_n = (qg_refs[s][:, HEAD_DIM:].astype(F32) * inv_rows).astype(BF)
        return inv, delta, q_n, g_n

    def back(s, c, state, dqt):
        _, delta, q_n, g_n = state
        rows = window(s, c)
        e = e_scs[s % 2][c * ROWS : (c + 1) * ROWS, :]
        ds = e * (dp_scs[s % 2][c * ROWS : (c + 1) * ROWS, :] - delta).astype(BF)
        dk[rows, :] += dot(ds, q_n)
        dv[rows, :] += dot(e, g_n)
        return dqt + dot(kt[:, rows], ds)

    state = None
    for s in range(group + 1):
        if s < group:
            shifts = scores(s)
            gt = qg_refs[s][:, HEAD_DIM:].T
            ot = jnp.zeros((vt.shape[0], ROWS), F32)
        dqt = jnp.zeros((HEAD_DIM, ROWS), F32)
        for c in range(chunks):
            if s < group:
                ot = weigh(s, c, shifts, gt, ot)
            if s:
                dqt = back(s - 1, c, state, dqt)
        if s:
            both_refs[s - 1][:, HEAD_DIM:] = (dqt * (state[0] * scale)).T.astype(BF)
        if s < group:
            state = settle(s, ot, gt)
    for b in range(blocks):
        for s in range(group):
            here = aligned((position[b] * group + (s ^ mine)) * ROWS, ROWS)
            out = out_refs[b]
            out[s * ROWS : (s + 1) * ROWS, :HEAD_DIM] = dk[here, :].astype(out.dtype)
            out[s * ROWS : (s + 1) * ROWS, HEAD_DIM:] = dv[here, :].astype(out.dtype)


def attend(place, kv, qg, before, head, heads, *, group, reach, radius, devices, sets):
    blocks = 2 * radius + 1
    size = group * ROWS
    span = blocks * size
    wide = 2 * HEAD_DIM
    keys = (2 * reach + 1) * ROWS
    pairs = size * keys

    def of(count):
        return pl.BlockSpec((count, wide), lambda i: (0, head))

    def fixed(*shape):
        return pl.BlockSpec(shape, lambda i: (0,) * len(shape))

    shape = jax.ShapeDtypeStruct
    return pl.pallas_call(
        functools.partial(attend_kernel, (group, reach, radius, devices, sets, len(before))),
        grid=(1,),
        out_shape=[shape((ROWS, heads * wide), BF)] * group
        + [shape((HEAD_DIM, size), BF)]
        + [shape((size, wide), F32 if b == 0 else BF) for b in range(blocks)],
        in_specs=[SMEM]
        + [of(len(members) * ROWS) for _ in range(blocks) for members in sets]
        + [of(ROWS)] * group
        + [HBM] * len(before),
        out_specs=[of(ROWS)] * group
        + [fixed(HEAD_DIM, size)]
        + [fixed(size, wide)] * blocks,
        scratch_shapes=[
            pltpu.VMEM((span, HEAD_DIM), BF),
            pltpu.VMEM((span, HEAD_DIM), BF),
            pltpu.VMEM((HEAD_DIM, span), BF),
            pltpu.VMEM((HEAD_DIM + 16, span), BF),
            pltpu.VMEM((keys, ROWS), F32),
            pltpu.VMEM((keys, ROWS), F32),
            pltpu.VMEM((keys, ROWS), F32),
            pltpu.VMEM((keys, ROWS), BF),
            pltpu.VMEM((keys, ROWS), BF),
            pltpu.VMEM((span, HEAD_DIM), F32),
            pltpu.VMEM((span, HEAD_DIM), F32),
        ],
        compiler_params=PARAMS,
        cost_estimate=pl.CostEstimate(
            flops=12 * pairs * HEAD_DIM, bytes_accessed=6 * size * wide * 2, transcendentals=pairs
        ),
        input_output_aliases={1 + blocks * len(sets) + group + i: i for i in range(len(before))},
    )(place, *[ref for refs in kv for ref in refs], *qg, *before)


def pack(place, arrays, group, heads):
    rows = arrays[0].shape[0]
    count = len(arrays)

    def kernel(place_ref, *refs):
        arrived = refs[-1]
        copies = []
        for s in range(group):
            for head in range(heads):
                for i in range(count):
                    at = (head * count + i) * HEAD_DIM
                    start = ((place_ref[0] ^ s) * heads + head) * HEAD_DIM
                    copies.append(
                        pltpu.make_async_copy(
                            refs[i].at[:, aligned(start, HEAD_DIM)],
                            refs[count + s].at[:, at : at + HEAD_DIM],
                            arrived.at[len(copies)],
                        )
                    )
        for copy in copies:
            copy.start()
        for copy in copies:
            copy.wait()

    return pl.pallas_call(
        kernel,
        out_shape=[jax.ShapeDtypeStruct((rows, heads * count * HEAD_DIM), BF)] * group,
        in_specs=[SMEM] + [HBM] * count,
        out_specs=[VMEM] * group,
        scratch_shapes=[pltpu.SemaphoreType.DMA((group * heads * count,))],
        compiler_params=PACK_PARAMS,
    )(place, *arrays)


def grad_own(place, own, weight, sides):
    rows, width = own.shape

    def kernel(place_ref, own_ref, w_ref, total_ref, *refs):
        first, arrived = refs[-2:]
        copies = []
        for j in range(sides):
            columns = aligned((place_ref[2] ^ j) * width, width)
            target = refs[j - 1] if j else first
            copies.append(pltpu.make_async_copy(w_ref.at[:, columns], target, arrived.at[j]))
        for copy in copies:
            copy.start()
        turned = own_ref[...].T
        copies[0].wait()
        total_ref[...] = dot(first[...], turned)
        for copy in copies[1:]:
            copy.wait()

    shape = jax.ShapeDtypeStruct
    return pl.pallas_call(
        kernel,
        out_shape=[shape((width, rows), F32)] + [shape((weight.shape[0], width), BF)] * (sides - 1),
        in_specs=[SMEM, VMEM, HBM],
        out_specs=[VMEM] * sides,
        scratch_shapes=[pltpu.VMEM((weight.shape[0], width), BF), pltpu.SemaphoreType.DMA((sides,))],
        compiler_params=PARAMS,
        cost_estimate=pl.CostEstimate(
            flops=2 * rows * width * width, bytes_accessed=2 * weight.size, transcendentals=0
        ),
    )(place, own, weight)


def grad_pack(place, queries, total, grads, weights, group, heads):
    rows, width = queries.shape
    sides = len(grads)

    def kernel(place_ref, q_ref, total_ref, *refs):
        turned_ref = refs[-1]
        total = total_ref[...]
        for j in range(sides):
            total = total + dot(refs[sides + j][...], refs[j][...].T)
        turned_ref[...] = total.astype(BF)
        for s in range(group):
            for head in range(heads):
                start = ((place_ref[0] ^ s) * heads + head) * HEAD_DIM
                at = 2 * head * HEAD_DIM
                here = aligned(start, HEAD_DIM)
                refs[2 * sides + s][:, at : at + HEAD_DIM] = q_ref[:, here]
                refs[2 * sides + s][:, at + HEAD_DIM : at + 2 * HEAD_DIM] = turned_ref[here, :].T

    return pl.pallas_call(
        kernel,
        out_shape=[jax.ShapeDtypeStruct((rows, heads * 2 * HEAD_DIM), BF)] * group,
        in_specs=[SMEM] + [VMEM] * (2 + 2 * sides),
        out_specs=[VMEM] * group,
        scratch_shapes=[pltpu.VMEM((width, rows), BF)],
        compiler_params=PARAMS,
        cost_estimate=pl.CostEstimate(
            flops=2 * rows * width * width * sides, bytes_accessed=2 * rows * width, transcendentals=0
        ),
    )(place, queries, total, *grads, *weights)


def mix(place, slots, weight, heads, sides):
    group = len(slots)
    rows = slots[0].shape[0]
    width = group * heads * HEAD_DIM

    def kernel(place_ref, w_ref, *refs):
        attn_ref, held, arrived = refs[-3:]
        shares, grad_ref = refs[group : group + sides], refs[group + sides]
        copies = []
        for j in range(sides):
            columns = aligned((place_ref[2] ^ j) * width, width)
            copies.append(pltpu.make_async_copy(w_ref.at[:, columns], held.at[j], arrived.at[j]))
        for copy in reversed(copies):
            copy.start()
        for s in range(group):
            for head in range(heads):
                here = aligned(((place_ref[0] ^ s) * heads + head) * HEAD_DIM, HEAD_DIM)
                at = 2 * head * HEAD_DIM
                attn_ref[:, here] = refs[s][:, at : at + HEAD_DIM]
                grad_ref[:, here] = refs[s][:, at + HEAD_DIM : at + 2 * HEAD_DIM]
        for j in reversed(range(sides)):
            copies[j].wait()
            shares[j][...] = dot(attn_ref[...], held[j]).astype(BF)

    shape = jax.ShapeDtypeStruct((rows, width), BF)
    return pl.pallas_call(
        kernel,
        out_shape=[shape] * (sides + 1),
        in_specs=[SMEM, HBM] + [VMEM] * group,
        out_specs=[VMEM] * (sides + 1),
        scratch_shapes=[
            pltpu.VMEM((rows, width), BF),
            pltpu.VMEM((sides, weight.shape[0], width), BF),
            pltpu.SemaphoreType.DMA((sides,)),
        ],
        compiler_params=PARAMS,
        cost_estimate=pl.CostEstimate(
            flops=2 * rows * width * width * sides, bytes_accessed=2 * weight.size, transcendentals=0
        ),
    )(place, weight, *slots)


def fold(place, kept, came, bit, narrow):
    rows, columns = kept.shape

    def kernel(place_ref, kept_ref, came_ref, away_ref, out_ref):
        own = (place_ref[1] // bit) % 2
        for i in range(columns // narrow // 2):
            there = slice(i * narrow, (i + 1) * narrow)
            away = aligned((2 * i + 1 - own) * narrow, narrow)
            here = aligned((2 * i + own) * narrow, narrow)
            away_ref[:, there] = (kept_ref[:, away] + came_ref[:, away].astype(F32)).astype(BF)
            out_ref[:, there] = kept_ref[:, here] + came_ref[:, here].astype(F32)

    shape = (rows, columns // 2)
    return pl.pallas_call(
        kernel,
        out_shape=[jax.ShapeDtypeStruct(shape, BF), jax.ShapeDtypeStruct(shape, F32)],
        in_specs=[SMEM, VMEM, VMEM],
        out_specs=[VMEM] * 2,
        compiler_params=PARAMS,
    )(place, kept, came)


def fold_last(place, kept, came, group):
    rows, columns = kept.shape
    share = columns // group

    def kernel(place_ref, kept_ref, came_ref, *refs):
        for s in range(group):
            here = aligned((place_ref[0] ^ s) * share, share)
            refs[s][...] = (kept_ref[:, here] + came_ref[:, here].astype(F32)).astype(BF)

    return pl.pallas_call(
        kernel,
        out_shape=[jax.ShapeDtypeStruct((rows, share), BF)] * group,
        in_specs=[SMEM, VMEM, VMEM],
        out_specs=[VMEM] * group,
        compiler_params=PARAMS,
    )(place, kept, came)


def stack(place, slots):
    group = len(slots)
    rows, columns = slots[0].shape

    def kernel(place_ref, *refs):
        for s in range(group):
            refs[group][aligned((place_ref[0] ^ s) * rows, rows), :] = refs[s][...]

    return pl.pallas_call(
        kernel,
        out_shape=jax.ShapeDtypeStruct((group * rows, columns), BF),
        in_specs=[SMEM] + [VMEM] * group,
        out_specs=VMEM,
        compiler_params=PARAMS,
    )(place, *slots)


def unpack(place, slots, heads):
    group = len(slots)
    flat = [piece for pieces in slots for piece in pieces]
    each = len(flat) // group
    rows = flat[0].shape[0]

    def kernel(place_ref, *refs):
        arrived = refs[-1]
        copies = []
        for s in range(group):
            for head in range(heads):
                source = refs[s * each + (head if each > 1 else 0)]
                base = 0 if each > 1 else 2 * head * HEAD_DIM
                start = ((place_ref[0] ^ s) * heads + head) * HEAD_DIM
                for i in range(2):
                    at = base + i * HEAD_DIM
                    copies.append(
                        pltpu.make_async_copy(
                            source.at[:, at : at + HEAD_DIM],
                            refs[len(flat) + i].at[:, aligned(start, HEAD_DIM)],
                            arrived.at[len(copies)],
                        )
                    )
        for copy in copies:
            copy.start()
        for copy in copies:
            copy.wait()

    return pl.pallas_call(
        kernel,
        out_shape=[jax.ShapeDtypeStruct((rows, group * heads * HEAD_DIM), BF)] * 2,
        in_specs=[SMEM] + [HBM] * len(flat),
        out_specs=[VMEM] * 2,
        scratch_shapes=[pltpu.SemaphoreType.DMA((2 * group * heads,))],
        compiler_params=PARAMS,
    )(place, *flat)


def add_slots(own, others, group):
    rows = own.shape[0] // group

    def kernel(own_ref, *refs):
        for s in range(group):
            here = slice(s * rows, (s + 1) * rows)
            total = own_ref[here, :]
            for ref in refs[: len(others)]:
                total = total + ref[here, :].astype(F32)
            refs[len(others) + s][...] = total.astype(BF)

    return pl.pallas_call(
        kernel,
        out_shape=[jax.ShapeDtypeStruct((rows, own.shape[1]), BF)] * group,
        in_specs=[VMEM] * (1 + len(others)),
        out_specs=[VMEM] * group,
        compiler_params=PARAMS,
    )(own, *others)


def weight_product(place, turned, grads, blocks):
    heads, group, sides = len(turned), len(grads), len(grads[0])
    rows, width = grads[0][0].shape
    narrow = sides * width // blocks
    many = width // narrow // 2
    pieces = [grads[s][j] for j in range(sides) for s in range(group)]

    def kernel(place_ref, *refs):
        own = place_ref[1] % 2
        away_ref, kept_ref = refs[heads + len(pieces) :]
        for j in range(sides):
            for i in range(many):
                there = aligned(((place_ref[2] ^ j) * many + i) * narrow, narrow)
                for kept in range(2):
                    at = aligned((2 * i + (own if kept else 1 - own)) * narrow, narrow)
                    for head in range(heads):
                        here = slice(head * HEAD_DIM, (head + 1) * HEAD_DIM)
                        total = None
                        for s in range(group):
                            one = dot(
                                refs[head][:, s * rows : (s + 1) * rows],
                                refs[heads + j * group + s][:, at],
                            )
                            total = one if total is None else total + one
                        if kept:
                            kept_ref[here, there] = total
                        else:
                            away_ref[here, there] = total.astype(BF)

    shape = (heads * HEAD_DIM, sides * width // 2)
    return pl.pallas_call(
        kernel,
        out_shape=[jax.ShapeDtypeStruct(shape, BF), jax.ShapeDtypeStruct(shape, F32)],
        in_specs=[SMEM] + [VMEM] * (heads + len(pieces)),
        out_specs=[VMEM] * 2,
        compiler_params=PARAMS,
        cost_estimate=pl.CostEstimate(
            flops=4 * heads * HEAD_DIM * group * rows * shape[1],
            bytes_accessed=4 * group * rows * shape[1],
            transcendentals=0,
        ),
    )(place, *turned, *pieces)


def swapped(piece, axis, mask):
    count = lax.axis_size(axis)
    return lax.ppermute(piece, axis, [(i, i ^ mask) for i in range(count)])


def paired(piece, distance, parity):
    count = lax.axis_size("block")
    lower = [i for i in range(count) if (i // distance) % 2 == parity and i + distance < count]
    route = [pair for i in lower for pair in ((i, i + distance), (i + distance, i))]
    return lax.ppermute(piece, "block", route)


def exchanged(slots):
    return [slots[0]] + [swapped(slots[s], "group", s) for s in range(1, len(slots))]


def placed_in_order(slots, mine, axis):
    size = slots[0].shape[axis]
    shape = list(slots[0].shape)
    shape[axis] = size * len(slots)
    whole = jnp.zeros(shape, slots[0].dtype)
    for s, slot in enumerate(slots):
        whole = lax.dynamic_update_slice_in_dim(whole, slot, (mine ^ s) * size, axis)
    return whole


def step(queries, keys, values, out_grad, out_weight):
    rows, width = queries.shape
    blocks, group, sides = (lax.axis_size(a) for a in ("block", "group", "heads"))
    block, mine, side = (lax.axis_index(a) for a in ("block", "group", "heads"))
    heads = width // HEAD_DIM // group
    part = heads * HEAD_DIM
    reach = (WIN + FR_DEV - 1) // FR_DEV
    radius = -(-reach // group)
    place = jnp.stack([mine, block, side]).astype(jnp.int32)
    half = max(group // 2, 1)
    sets = [tuple(s) for s in (range(half), range(half, group)) if len(s)]
    pairs = [(d, parity) for d in range(1, radius + 1) for parity in range(2)]

    grads = {0: [out_grad] + [swapped(out_grad, "heads", j) for j in range(1, sides)]}
    kv_slots = exchanged(pack(place, (keys, values), group, heads))
    near = [[None] * len(sets) for _ in range(2 * radius + 1)]
    for i, members in enumerate(sets):
        kv = jnp.concatenate([kv_slots[s] for s in members], axis=0)
        near[0][i] = kv
        for b, (d, parity) in enumerate(pairs):
            near[b + 1][i] = paired(kv, d, parity)
    total, *others = grad_own(place, out_grad, out_weight, sides)
    qg_slots = exchanged(grad_pack(place, queries, total, grads[0][1:], others, group, heads))
    bit = group // 2
    while bit:
        for s in list(grads):
            if bit > 1:
                first = swapped(grads[s][0], "group", bit)
                rest = [swapped(first, "heads", j) for j in range(1, sides)]
                grads[s ^ bit] = [first] + rest
            else:
                grads[s ^ bit] = [swapped(piece, "group", bit) for piece in grads[s]]
        bit //= 2
    grads = [grads[s] for s in range(group)]

    results = []
    turned = []
    totals = [[] for _ in range(group)]
    for head in range(heads):
        outs = attend(
            place, near, qg_slots, results, head, heads,
            group=group, reach=reach, radius=radius, devices=blocks * group, sets=sets,
        )
        results, turn, dkv = outs[:group], outs[group], outs[group + 1 :]
        turned.append(turn)
        came = [paired(dkv[b + 1], d, parity) for b, (d, parity) in enumerate(pairs)]
        sums = add_slots(dkv[0], came, group)
        for s, total in enumerate(exchanged(sums)):
            totals[s].append(total)
    results = exchanged(results)
    *shares, query_grad = mix(place, results, out_weight, heads, sides)
    mixed = shares[0].astype(F32)
    for j in range(1, sides):
        mixed = mixed + swapped(shares[j], "heads", j).astype(F32)
    key_grad, value_grad = unpack(place, totals, heads)

    narrow = width * sides // blocks
    share = narrow // group
    if share % HEAD_DIM == 0 and width % (2 * narrow) == 0:
        away, kept = weight_product(place, turned, grads, blocks)
        bit = 1
        while 2 * bit < blocks:
            came = swapped(away, "block", bit)
            bit *= 2
            away, kept = fold(place, kept, came, bit, narrow)
        came = swapped(away, "block", bit)
        slots = fold_last(place, kept, came, group)
        weight_grad = stack(place, exchanged(slots))
    else:
        partial = sum(
            jnp.dot(
                jnp.concatenate([t[:, s * rows : (s + 1) * rows] for t in turned], axis=0),
                placed_in_order(grads[s], side, 1),
                preferred_element_type=F32,
            )
            for s in range(group)
        )
        bit = 1
        partial = partial.reshape(part, blocks, narrow)
        while bit < blocks:
            halves = partial.reshape(part, partial.shape[1] // 2, 2, narrow)
            own = (block // bit) % 2
            away = lax.dynamic_index_in_dim(halves, 1 - own, 2, keepdims=False).astype(BF)
            kept = lax.dynamic_index_in_dim(halves, own, 2, keepdims=False)
            partial = kept + swapped(away, "block", bit).astype(F32)
            bit *= 2
        partial = partial.reshape(part, narrow).astype(BF)
        slots = [
            lax.dynamic_slice_in_dim(partial, (mine ^ s) * share, share, 1) for s in range(group)
        ]
        weight_grad = placed_in_order(exchanged(slots), mine, 0)
    return mixed.astype(BF), query_grad, key_grad, value_grad, weight_grad


def solution(mesh):
    devices, sides = mesh.devices.shape
    reach = (WIN + FR_DEV - 1) // FR_DEV

    def run(queries, keys, values, out_grad, out_weight):
        heads = queries.shape[1] // sides // HEAD_DIM
        group = 1
        while 2 * group <= reach and heads % (2 * group) == 0 and devices % (2 * group) == 0:
            group *= 2
        fine = Mesh(
            mesh.devices.reshape(devices // group, group, sides), ("block", "group", "heads")
        )
        split = P(("block", "group"), "heads")
        return jax.shard_map(
            step,
            mesh=fine,
            in_specs=(split, split, split, split, P("heads", None)),
            out_specs=(split, split, split, split, P("heads", ("block", "group"))),
            check_vma=False,
        )(queries, keys, values, out_grad, out_weight)

    return run
```

```python
import functools

import jax
import jax.numpy as jnp
from jax import lax
from jax.experimental import pallas as pl
from jax.experimental.pallas import tpu as pltpu
from jax.sharding import Mesh
from jax.sharding import PartitionSpec as P


HEAD_DIM = 128
REGIONS = 128
WIN = 8
FR_DEV = 2
ROWS = FR_DEV * REGIONS
LOW = -1e30
LOG2E = 1.4426950408889634
PLAIN = (((1,), (0,)), ((), ()))
BF, F32 = jnp.bfloat16, jnp.float32
VMEM = pl.BlockSpec(memory_space=pltpu.VMEM)
HBM = pl.BlockSpec(memory_space=pltpu.HBM)
PARAMS = pltpu.CompilerParams(vmem_limit_bytes=48 * 1024 * 1024)

EVEN_PARAMS = pltpu.CompilerParams(vmem_limit_bytes=48 * 1024 * 1024)
PACK_PARAMS = pltpu.CompilerParams(vmem_limit_bytes=48 * 1024 * 1024)


def dot(a, b, dims=PLAIN):
    return lax.dot_general(a, b, dims, preferred_element_type=F32)


def located():
    return [lax.axis_index(name) for name in ("group", "block", "heads")]


def aligned(start, size):
    return pl.ds(pl.multiple_of(start, size), size)


def attend_kernel(cfg, *refs):
    group, reach, radius, devices, filled, head = cfg
    blocks = 2 * radius + 1
    refs = list(refs)

    def take(count):
        head, refs[:] = refs[:count], refs[count:]
        return head

    kv_refs = take(blocks)
    qg_refs = take(group)
    done_refs = take(filled)
    both_refs = take(group)
    (turned_ref,) = take(1)
    out_refs = take(blocks)
    kw, vw, kt, vt, s_sc, *rest = refs
    dp_scs, e_scs, (dk, dv) = rest[:2], rest[2:4], rest[4:]
    mine, block, _ = located()
    base = 2 * HEAD_DIM * head
    left, right = slice(base, base + HEAD_DIM), slice(base + HEAD_DIM, base + 2 * HEAD_DIM)
    for done, both in zip(done_refs, both_refs):
        both[:, :base] = done[:, :base]
    scale = HEAD_DIM ** -0.5
    chunks = 2 * reach + 1
    dk[...] = jnp.zeros_like(dk)
    dv[...] = jnp.zeros_like(dv)
    vt[HEAD_DIM:, :] = jnp.ones((vt.shape[0] - HEAD_DIM, vt.shape[1]), vt.dtype)
    position = [radius]
    for d in range(1, radius + 1):
        for parity in range(2):
            position.append(radius + jnp.where((block // d) % 2 == parity, d, -d))
    for b in range(blocks):
        for s in range(group):
            there = aligned((position[b] * group + (s ^ mine)) * ROWS, ROWS)
            k = kv_refs[b][s * ROWS : (s + 1) * ROWS, :HEAD_DIM]
            v = kv_refs[b][s * ROWS : (s + 1) * ROWS, HEAD_DIM:]
            kw[there, :] = k
            vw[there, :] = v
            kt[:, there] = k.T
            vt[:HEAD_DIM, there] = v.T
    query_frame = lax.broadcasted_iota(jnp.int32, (1, ROWS), 1) // REGIONS

    def window(s, c):
        return aligned(((s ^ mine) + radius * group - reach + c) * ROWS, ROWS)

    def scores(s):
        qt = qg_refs[s][:, :HEAD_DIM].T
        top = jnp.full((1, ROWS), LOW, F32)
        biases = []
        for c in range(chunks):
            st = dot(kw[window(s, c), :], qt)
            s_sc[c * ROWS : (c + 1) * ROWS, :] = st
            device = block * group + (s ^ mine) + (c - reach)
            live = jnp.where((device >= 0) & (device < devices), 0.0, LOW)
            for f in range(FR_DEV):
                distance = (c - reach) * FR_DEV + f - query_frame
                bias = jnp.where(jnp.abs(distance) <= WIN, live, LOW)
                biases.append(bias)
                some = st[f * REGIONS : (f + 1) * REGIONS, :]
                top = jnp.maximum(top, jnp.max(some, axis=0, keepdims=True) * (scale * LOG2E) + bias)
        return [bias - top for bias in biases]

    def weigh(s, c, shifts, gt, ot):
        e_sc, dp_sc = e_scs[s % 2], dp_scs[s % 2]
        for f in range(FR_DEV):
            some = slice(c * ROWS + f * REGIONS, c * ROWS + (f + 1) * REGIONS)
            e_sc[some, :] = jnp.exp2(
                s_sc[some, :] * (scale * LOG2E) + shifts[c * FR_DEV + f]
            ).astype(BF)
        dp_sc[c * ROWS : (c + 1) * ROWS, :] = dot(vw[window(s, c), :], gt)
        return ot + dot(vt[:, window(s, c)], e_sc[c * ROWS : (c + 1) * ROWS, :])

    def settle(s, ot, gt):
        inv = 1.0 / ot[HEAD_DIM : HEAD_DIM + 1, :]
        ot = ot[:HEAD_DIM, :] * inv
        delta = jnp.sum(ot * gt.astype(F32), axis=0, keepdims=True)
        turned_ref[:, s * ROWS : (s + 1) * ROWS] = ot.astype(BF)
        both_refs[s][:, left] = ot.T.astype(BF)
        inv_rows = jnp.broadcast_to(inv, (HEAD_DIM, ROWS)).T
        q_n = (qg_refs[s][:, :HEAD_DIM].astype(F32) * (inv_rows * scale)).astype(BF)
        g_n = (qg_refs[s][:, HEAD_DIM:].astype(F32) * inv_rows).astype(BF)
        return inv, delta, q_n, g_n

    def back(s, c, state, dqt):
        _, delta, q_n, g_n = state
        rows = window(s, c)
        e = e_scs[s % 2][c * ROWS : (c + 1) * ROWS, :]
        ds = e * (dp_scs[s % 2][c * ROWS : (c + 1) * ROWS, :] - delta).astype(BF)
        dk[rows, :] += dot(ds, q_n)
        dv[rows, :] += dot(e, g_n)
        return dqt + dot(kt[:, rows], ds)

    state = None
    for s in range(group + 1):
        if s < group:
            shifts = scores(s)
            gt = qg_refs[s][:, HEAD_DIM:].T
            ot = jnp.zeros((vt.shape[0], ROWS), F32)
        dqt = jnp.zeros((HEAD_DIM, ROWS), F32)
        for c in range(chunks):
            if s < group:
                ot = weigh(s, c, shifts, gt, ot)
            if s:
                dqt = back(s - 1, c, state, dqt)
        if s:
            both_refs[s - 1][:, right] = (dqt * (state[0] * scale)).T.astype(BF)
        if s < group:
            state = settle(s, ot, gt)
    for b in range(blocks):
        for s in range(group):
            here = aligned((position[b] * group + (s ^ mine)) * ROWS, ROWS)
            out = out_refs[b]
            out[s * ROWS : (s + 1) * ROWS, :HEAD_DIM] = dk[here, :].astype(out.dtype)
            out[s * ROWS : (s + 1) * ROWS, HEAD_DIM:] = dv[here, :].astype(out.dtype)


def attend(kv, qg, before, head, heads, *, group, reach, radius, devices):
    blocks = 2 * radius + 1
    size = group * ROWS
    span = blocks * size
    wide = 2 * HEAD_DIM
    keys = (2 * reach + 1) * ROWS
    pairs = size * keys

    shape = jax.ShapeDtypeStruct
    return pl.pallas_call(
        functools.partial(attend_kernel, (group, reach, radius, devices, len(before), head)),
        out_shape=[shape((ROWS, heads * wide), BF)] * group
        + [shape((HEAD_DIM, size), BF)]
        + [shape((size, wide), F32 if b == 0 else BF) for b in range(blocks)],
        in_specs=[VMEM] * (blocks + group + len(before)),
        out_specs=[VMEM] * (group + 1 + blocks),
        scratch_shapes=[
            pltpu.VMEM((span, HEAD_DIM), BF),
            pltpu.VMEM((span, HEAD_DIM), BF),
            pltpu.VMEM((HEAD_DIM, span), BF),
            pltpu.VMEM((HEAD_DIM + 16, span), BF),
            pltpu.VMEM((keys, ROWS), F32),
            pltpu.VMEM((keys, ROWS), F32),
            pltpu.VMEM((keys, ROWS), F32),
            pltpu.VMEM((keys, ROWS), BF),
            pltpu.VMEM((keys, ROWS), BF),
            pltpu.VMEM((span, HEAD_DIM), F32),
            pltpu.VMEM((span, HEAD_DIM), F32),
        ],
        compiler_params=EVEN_PARAMS,
        cost_estimate=pl.CostEstimate(
            flops=12 * pairs * HEAD_DIM, bytes_accessed=6 * size * wide * 2, transcendentals=pairs
        ),
    )(*kv, *qg, *before)


def pack(arrays, group, heads):
    rows = arrays[0].shape[0]
    count = len(arrays)

    def kernel(*refs):
        place = located()
        arrived = refs[-1]
        copies = []
        for s in range(group):
            for head in range(heads):
                for i in range(count):
                    at = i * HEAD_DIM
                    start = ((place[0] ^ s) * heads + head) * HEAD_DIM
                    copies.append(
                        pltpu.make_async_copy(
                            refs[i].at[:, aligned(start, HEAD_DIM)],
                            refs[count + head * group + s].at[:, at : at + HEAD_DIM],
                            arrived.at[len(copies)],
                        )
                    )
        for copy in copies:
            copy.start()
        for copy in copies:
            copy.wait()

    return pl.pallas_call(
        kernel,
        out_shape=[jax.ShapeDtypeStruct((rows, count * HEAD_DIM), BF)] * (heads * group),
        in_specs=[HBM] * count,
        out_specs=[VMEM] * (heads * group),
        scratch_shapes=[pltpu.SemaphoreType.DMA((group * heads * count,))],
        compiler_params=PACK_PARAMS,
    )(*arrays)


def grad_own(own, weight, sides):
    rows, width = own.shape

    def kernel(own_ref, w_ref, total_ref, *refs):
        place = located()
        first, arrived = refs[-2:]
        copies = []
        for j in range(sides):
            columns = aligned((place[2] ^ j) * width, width)
            target = refs[j - 1] if j else first
            copies.append(pltpu.make_async_copy(w_ref.at[:, columns], target, arrived.at[j]))
        for copy in copies:
            copy.start()
        turned = own_ref[...].T
        copies[0].wait()
        total_ref[...] = dot(first[...], turned)
        for copy in copies[1:]:
            copy.wait()

    shape = jax.ShapeDtypeStruct
    return pl.pallas_call(
        kernel,
        out_shape=[shape((width, rows), F32)] + [shape((weight.shape[0], width), BF)] * (sides - 1),
        in_specs=[VMEM, HBM],
        out_specs=[VMEM] * sides,
        scratch_shapes=[pltpu.VMEM((weight.shape[0], width), BF), pltpu.SemaphoreType.DMA((sides,))],
        compiler_params=PARAMS,
        cost_estimate=pl.CostEstimate(
            flops=2 * rows * width * width, bytes_accessed=2 * weight.size, transcendentals=0
        ),
    )(own, weight)


def grad_pack(queries, total, grads, weights, group, heads):
    rows, width = queries.shape
    sides = len(grads) + 1

    def kernel(q_ref, total_ref, *refs):
        place = located()
        turned_ref = refs[-1]
        total = total_ref[...]
        for j in range(sides - 1):
            total = total + dot(refs[sides - 1 + j][...], refs[j][...].T)
        turned_ref[...] = total.astype(BF)
        for s in range(group):
            for head in range(heads):
                start = ((place[0] ^ s) * heads + head) * HEAD_DIM
                out = refs[2 * (sides - 1) + head * group + s]
                here = aligned(start, HEAD_DIM)
                out[:, :HEAD_DIM] = q_ref[:, here]
                out[:, HEAD_DIM:] = turned_ref[here, :].T

    return pl.pallas_call(
        kernel,
        out_shape=[jax.ShapeDtypeStruct((rows, 2 * HEAD_DIM), BF)] * (heads * group),
        in_specs=[VMEM] * (2 * sides),
        out_specs=[VMEM] * (heads * group),
        scratch_shapes=[pltpu.VMEM((width, rows), BF)],
        compiler_params=PARAMS,
        cost_estimate=pl.CostEstimate(
            flops=2 * rows * width * width * (sides - 1), bytes_accessed=2 * rows * width, transcendentals=0
        ),
    )(queries, total, *grads, *weights)


def mix(slots, weight, heads, sides):
    group = len(slots)
    rows = slots[0].shape[0]
    width = group * heads * HEAD_DIM

    def kernel(w_ref, *refs):
        place = located()
        attn_ref, held, arrived = refs[-3:]
        shares, grad_ref = refs[group : group + sides], refs[group + sides]
        copies = []
        for j in range(sides):
            columns = aligned((place[2] ^ j) * width, width)
            copies.append(pltpu.make_async_copy(w_ref.at[:, columns], held.at[j], arrived.at[j]))
        for copy in reversed(copies):
            copy.start()
        for s in range(group):
            for head in range(heads):
                here = aligned(((place[0] ^ s) * heads + head) * HEAD_DIM, HEAD_DIM)
                at = 2 * head * HEAD_DIM
                attn_ref[:, here] = refs[s][:, at : at + HEAD_DIM]
                grad_ref[:, here] = refs[s][:, at + HEAD_DIM : at + 2 * HEAD_DIM]
        for j in reversed(range(sides)):
            copies[j].wait()
            shares[j][...] = dot(attn_ref[...], held[j]).astype(BF)

    shape = jax.ShapeDtypeStruct((rows, width), BF)
    return pl.pallas_call(
        kernel,
        out_shape=[shape] * (sides + 1),
        in_specs=[HBM] + [VMEM] * group,
        out_specs=[VMEM] * (sides + 1),
        scratch_shapes=[
            pltpu.VMEM((rows, width), BF),
            pltpu.VMEM((sides, weight.shape[0], width), BF),
            pltpu.SemaphoreType.DMA((sides,)),
        ],
        compiler_params=PARAMS,
        cost_estimate=pl.CostEstimate(
            flops=2 * rows * width * width * sides, bytes_accessed=2 * weight.size, transcendentals=0
        ),
    )(weight, *slots)


def fold(kept, came, bit, narrow):
    rows, columns = kept.shape

    def kernel(kept_ref, came_ref, away_ref, out_ref):
        place = located()
        own = (place[1] // bit) % 2
        for i in range(columns // narrow // 2):
            there = slice(i * narrow, (i + 1) * narrow)
            away = aligned((2 * i + 1 - own) * narrow, narrow)
            here = aligned((2 * i + own) * narrow, narrow)
            away_ref[:, there] = (kept_ref[:, away] + came_ref[:, away].astype(F32)).astype(BF)
            out_ref[:, there] = kept_ref[:, here] + came_ref[:, here].astype(F32)

    shape = (rows, columns // 2)
    return pl.pallas_call(
        kernel,
        out_shape=[jax.ShapeDtypeStruct(shape, BF), jax.ShapeDtypeStruct(shape, F32)],
        in_specs=[VMEM, VMEM],
        out_specs=[VMEM] * 2,
        compiler_params=PARAMS,
    )(kept, came)


def fold_last(kept, came, group):
    rows, columns = kept[0].shape
    share = columns // group
    heads = len(kept)

    def kernel(*refs):
        place = located()
        for s in range(group):
            here = aligned((place[0] ^ s) * share, share)
            for head in range(heads):
                total = refs[head][:, here] + refs[heads + head][:, here].astype(F32)
                refs[2 * heads + s][head * rows : (head + 1) * rows, :] = total.astype(BF)

    return pl.pallas_call(
        kernel,
        out_shape=[jax.ShapeDtypeStruct((heads * rows, share), BF)] * group,
        in_specs=[VMEM] * (2 * heads),
        out_specs=[VMEM] * group,
        compiler_params=PARAMS,
    )(*kept, *came)


def stack(slots):
    group = len(slots)
    rows, columns = slots[0].shape

    def kernel(*refs):
        place = located()
        for s in range(group):
            refs[group][aligned((place[0] ^ s) * rows, rows), :] = refs[s][...]

    return pl.pallas_call(
        kernel,
        out_shape=jax.ShapeDtypeStruct((group * rows, columns), BF),
        in_specs=[VMEM] * group,
        out_specs=VMEM,
        compiler_params=PARAMS,
    )(*slots)


def unpack(slots, heads):
    group = len(slots)
    flat = [piece for pieces in slots for piece in pieces]
    each = len(flat) // group
    rows = flat[0].shape[0]

    def kernel(*refs):
        place = located()
        arrived = refs[-1]
        copies = []
        for s in range(group):
            for head in range(heads):
                source = refs[s * each + (head if each > 1 else 0)]
                base = 0 if each > 1 else 2 * head * HEAD_DIM
                start = ((place[0] ^ s) * heads + head) * HEAD_DIM
                for i in range(2):
                    at = base + i * HEAD_DIM
                    copies.append(
                        pltpu.make_async_copy(
                            source.at[:, at : at + HEAD_DIM],
                            refs[len(flat) + i].at[:, aligned(start, HEAD_DIM)],
                            arrived.at[len(copies)],
                        )
                    )
        for copy in copies:
            copy.start()
        for copy in copies:
            copy.wait()

    return pl.pallas_call(
        kernel,
        out_shape=[jax.ShapeDtypeStruct((rows, group * heads * HEAD_DIM), BF)] * 2,
        in_specs=[HBM] * len(flat),
        out_specs=[VMEM] * 2,
        scratch_shapes=[pltpu.SemaphoreType.DMA((2 * group * heads,))],
        compiler_params=PARAMS,
    )(*flat)


def add_slots(own, others, group):
    rows = own.shape[0] // group

    def kernel(own_ref, *refs):
        for s in range(group):
            here = slice(s * rows, (s + 1) * rows)
            total = own_ref[here, :]
            for ref in refs[: len(others)]:
                total = total + ref[here, :].astype(F32)
            refs[len(others) + s][...] = total.astype(BF)

    return pl.pallas_call(
        kernel,
        out_shape=[jax.ShapeDtypeStruct((rows, own.shape[1]), BF)] * group,
        in_specs=[VMEM] * (1 + len(others)),
        out_specs=[VMEM] * group,
        compiler_params=PARAMS,
    )(own, *others)


def weight_product(turned, grads, blocks):
    heads, group, sides = len(turned), len(grads), len(grads[0])
    rows, width = grads[0][0].shape
    narrow = sides * width // blocks
    many = width // narrow // 2
    pieces = [grads[s][j] for j in range(sides) for s in range(group)]

    def kernel(*refs):
        place = located()
        own = place[1] % 2
        outs = refs[heads + len(pieces) :]
        for j in range(sides):
            for i in range(many):
                there = aligned(((place[2] ^ j) * many + i) * narrow, narrow)
                for kept in range(2):
                    at = aligned((2 * i + (own if kept else 1 - own)) * narrow, narrow)
                    for head in range(heads):
                        total = None
                        for s in range(group):
                            one = dot(
                                refs[head][:, s * rows : (s + 1) * rows],
                                refs[heads + j * group + s][:, at],
                            )
                            total = one if total is None else total + one
                        if kept:
                            outs[heads + head][:, there] = total
                        else:
                            outs[head][:, there] = total.astype(BF)

    shape = (HEAD_DIM, sides * width // 2)
    return pl.pallas_call(
        kernel,
        out_shape=[jax.ShapeDtypeStruct(shape, BF)] * heads + [jax.ShapeDtypeStruct(shape, F32)] * heads,
        in_specs=[VMEM] * (heads + len(pieces)),
        out_specs=[VMEM] * (2 * heads),
        compiler_params=PARAMS,
        cost_estimate=pl.CostEstimate(
            flops=4 * heads * HEAD_DIM * group * rows * shape[1],
            bytes_accessed=4 * group * rows * shape[1],
            transcendentals=0,
        ),
    )(*turned, *pieces)


def swapped(piece, axis, mask):
    count = lax.axis_size(axis)
    return lax.ppermute(piece, axis, [(i, i ^ mask) for i in range(count)])


def paired(piece, distance, parity):
    count = lax.axis_size("block")
    lower = [i for i in range(count) if (i // distance) % 2 == parity and i + distance < count]
    route = [pair for i in lower for pair in ((i, i + distance), (i + distance, i))]
    return lax.ppermute(piece, "block", route)


def exchanged(slots):
    return [slots[0]] + [swapped(slots[s], "group", s) for s in range(1, len(slots))]


def placed_in_order(slots, mine, axis):
    size = slots[0].shape[axis]
    shape = list(slots[0].shape)
    shape[axis] = size * len(slots)
    whole = jnp.zeros(shape, slots[0].dtype)
    for s, slot in enumerate(slots):
        whole = lax.dynamic_update_slice_in_dim(whole, slot, (mine ^ s) * size, axis)
    return whole


def step(queries, keys, values, out_grad, out_weight):
    rows, width = queries.shape
    blocks, group, sides = (lax.axis_size(a) for a in ("block", "group", "heads"))
    block, mine, side = (lax.axis_index(a) for a in ("block", "group", "heads"))
    heads = width // HEAD_DIM // group
    part = heads * HEAD_DIM
    reach = (WIN + FR_DEV - 1) // FR_DEV
    radius = -(-reach // group)
    pairs = [(d, parity) for d in range(1, radius + 1) for parity in range(2)]

    grads = {0: [out_grad] + [swapped(out_grad, "heads", j) for j in range(1, sides)]}
    packed = pack((keys, values), group, heads)
    near = []
    for head in range(heads):
        slots = exchanged(packed[head * group : (head + 1) * group])
        kv = jnp.concatenate(slots, axis=0)
        near.append([kv] + [paired(kv, d, parity) for d, parity in pairs])
    total, *others = grad_own(out_grad, out_weight, sides)
    packed = grad_pack(queries, total, grads[0][1:], others, group, heads)
    qg_slots = [exchanged(packed[head * group : (head + 1) * group]) for head in range(heads)]
    bit = group // 2
    while bit:
        for s in list(grads):
            if bit > 1:
                first = swapped(grads[s][0], "group", bit)
                rest = [swapped(first, "heads", j) for j in range(1, sides)]
                grads[s ^ bit] = [first] + rest
            else:
                grads[s ^ bit] = [swapped(piece, "group", bit) for piece in grads[s]]
        bit //= 2
    grads = [grads[s] for s in range(group)]

    results = []
    turned = []
    totals = [[] for _ in range(group)]
    for head in range(heads):
        outs = attend(
            near[head], qg_slots[head], results, head, heads,
            group=group, reach=reach, radius=radius, devices=blocks * group,
        )
        results, turn, dkv = outs[:group], outs[group], outs[group + 1 :]
        turned.append(turn)
        came = [paired(dkv[b + 1], d, parity) for b, (d, parity) in enumerate(pairs)]
        sums = add_slots(dkv[0], came, group)
        for s, total in enumerate(exchanged(sums)):
            totals[s].append(total)
    results = exchanged(results)
    *shares, query_grad = mix(results, out_weight, heads, sides)
    came = [swapped(shares[j], "heads", j) for j in range(1, sides)]
    mixed = sum([piece.astype(F32) for piece in came], shares[0].astype(F32)).astype(BF)
    key_grad, value_grad = unpack(totals, heads)

    narrow = width * sides // blocks
    share = narrow // group
    if share % HEAD_DIM == 0 and width % (2 * narrow) == 0:
        outs = weight_product(turned, grads, blocks)
        away, kept = list(outs[:heads]), list(outs[heads:])
        bit = 1
        while 2 * bit < blocks:
            came = [swapped(away[h], "block", bit) for h in range(heads)]
            bit *= 2
            for h in range(heads):
                away[h], kept[h] = fold(kept[h], came[h], bit, narrow)
        came = [swapped(away[h], "block", bit) for h in range(heads)]
        slots = fold_last(kept, came, group)
        weight_grad = stack(exchanged(slots))
    else:
        partial = sum(
            jnp.dot(
                jnp.concatenate([t[:, s * rows : (s + 1) * rows] for t in turned], axis=0),
                placed_in_order(grads[s], side, 1),
                preferred_element_type=F32,
            )
            for s in range(group)
        )
        bit = 1
        partial = partial.reshape(part, blocks, narrow)
        while bit < blocks:
            halves = partial.reshape(part, partial.shape[1] // 2, 2, narrow)
            own = (block // bit) % 2
            away = lax.dynamic_index_in_dim(halves, 1 - own, 2, keepdims=False).astype(BF)
            kept = lax.dynamic_index_in_dim(halves, own, 2, keepdims=False)
            partial = kept + swapped(away, "block", bit).astype(F32)
            bit *= 2
        partial = partial.reshape(part, narrow).astype(BF)
        slots = [
            lax.dynamic_slice_in_dim(partial, (mine ^ s) * share, share, 1) for s in range(group)
        ]
        weight_grad = placed_in_order(exchanged(slots), mine, 0)
    return mixed, query_grad, key_grad, value_grad, weight_grad


def solution(mesh):
    devices, sides = mesh.devices.shape
    reach = (WIN + FR_DEV - 1) // FR_DEV

    def run(queries, keys, values, out_grad, out_weight):
        heads = queries.shape[1] // sides // HEAD_DIM
        group = 1
        while 2 * group <= reach and heads % (2 * group) == 0 and devices % (2 * group) == 0:
            group *= 2
        fine = Mesh(
            mesh.devices.reshape(devices // group, group, sides), ("block", "group", "heads")
        )
        split = P(("block", "group"), "heads")
        return jax.shard_map(
            step,
            mesh=fine,
            in_specs=(split, split, split, split, P("heads", None)),
            out_specs=(split, split, split, split, P("heads", ("block", "group"))),
            check_vma=False,
        )(queries, keys, values, out_grad, out_weight)

    return run
```
